256 devices in a mesh: ctx: 32 (over z, x), grp: 8 (over y, core).
Axes of the slice: x: 4, y: 4, z: 8, core: 2. Of those that a mesh axis runs over, the one named last changes fastest.
Arguments:
- query: bfloat16 [512, 5120], P('ctx', 'grp'), may hold values from -8 to 8
- keys: bfloat16 [131072, 1024], P('ctx', 'grp'), may hold values from -16 to 16
- values: bfloat16 [131072, 1024], P('ctx', 'grp'), may hold values from -6 to 6
- blocks: int32 [512, 32, 8], P(None, 'ctx'), may hold values from 0 to 31, as said below
Outputs:
- attended: bfloat16 [512, 5120], P(('ctx', 'grp'))
The draws below stay inside these ranges and needn't reach their ends.
Inputs may be any that keep to these rules, and one draw needn't show every extreme that they name: Each row's list for each context shard names 8 different blocks, the first of them block 0.
All inputs are finite; a program needn't handle non-finite values.
Results may differ from the reference program's by a relative error of at most 0.012.
Values may be sent and summed in bfloat16 or wider, within the bound.
No kernel may reach another device: no remote copies, remote signals or barrier semaphores. Data moves between devices by JAX's collectives and lax.ppermute only.
A program may use at most 192 MiB of HBM per device.

```python
import math
import jax
import jax.numpy as jnp
from jax import lax

HD = 128
QPK = 5
KVH = 8
QH = 40
ROWS = 512
CTX_DEV = 4096
CTXLEN = 131072
BLOCK = 128
BLK_DEV = 32
SEL = 8


def draw_query(key, part):
    noise_key = jax.random.fold_in(key, 1)
    base = jnp.clip(jax.random.normal(noise_key, (ROWS, QH * HD), jnp.float32), -6.0, 6.0)
    return base.astype(jnp.bfloat16)


def draw_keys(key, part):
    noise_key = jax.random.fold_in(key, 2)
    base = jnp.clip(2.5 * jax.random.normal(noise_key, (CTXLEN, KVH * HD), jnp.float32), -15.0, 15.0)
    return base.astype(jnp.bfloat16)


def draw_blocks(key, part):
    shard_count = CTXLEN // CTX_DEV
    random_bits = jax.random.randint(jax.random.fold_in(key, 3), (ROWS, shard_count, BLK_DEV - 1), 0, 1 << 20)
    distinct = random_bits * BLK_DEV + jnp.arange(BLK_DEV - 1, dtype=jnp.int32)[None, None, :]
    unused, chosen = lax.top_k(distinct, SEL - 1)
    first_block = jnp.zeros((ROWS, shard_count, 1), jnp.int32)
    return jnp.concatenate([first_block, chosen.astype(jnp.int32) + 1], axis=2)


def block_scale(rng, dims, split, smallest, high):
    def one(position, parts):
        draws = jax.random.uniform(jax.random.fold_in(jax.random.fold_in(rng, 6), position), (parts,), jnp.float32, smallest / len(split), high / len(split))
        return jnp.repeat(jnp.exp(draws), dims[position] // parts).reshape((-1,) + (1,) * (len(dims) - position - 1))

    gain = one(*split[0])
    for cut in split[1:]:
        gain = gain * one(*cut)
    return gain


def normal_values(own_key, dims, scale, most, shards=(), kind=jnp.bfloat16):
    values = scale * jax.random.normal(own_key, dims, jnp.float32)
    if shards:
        values = values * block_scale(own_key, dims, shards, -0.22, 0.18)
    return jnp.clip(values, -most, most).astype(kind)


def setup_inputs(seed: int = 0) -> dict:
    splits = jax.random.split(jax.random.key(seed), 5)
    return {
        "query": draw_query(jax.random.fold_in(splits[4], 71), 0),
        "keys": draw_keys(jax.random.fold_in(splits[4], 71), 0),
        "values": normal_values(splits[2], (CTXLEN, KVH * HD), 1.0, 6.0, ((0, 32), (1, 8))),
        "blocks": draw_blocks(jax.random.fold_in(splits[4], 71), 0),
    }


def reference(query, keys, values, blocks):
    shard_count = CTXLEN // CTX_DEV
    score_scale = 1.0 / math.sqrt(HD)
    query_all = query.astype(jnp.float32).reshape(ROWS, KVH, QPK, HD)

    def one_shard(shard):
        start = (shard * CTX_DEV).astype(jnp.int32)
        key_part = lax.dynamic_slice_in_dim(keys, start, CTX_DEV, 0).astype(jnp.float32).reshape(CTX_DEV, KVH, HD)
        value_part = lax.dynamic_slice_in_dim(values, start, CTX_DEV, 0).astype(jnp.float32).reshape(CTX_DEV, KVH, HD)
        listed_here = lax.dynamic_slice_in_dim(blocks, shard.astype(jnp.int32), 1, 1)[:, 0, :]
        block_ids = jnp.arange(BLK_DEV, dtype=jnp.int32)
        block_hits = jnp.any(listed_here[:, :, None] == block_ids[None, None, :], axis=1)
        token_mask = jnp.repeat(block_hits, BLOCK, axis=1)[:, None, None, :]
        scores = jnp.einsum('rgqd,tgd->rgqt', query_all, key_part) * score_scale
        local_max = lax.optimization_barrier(jnp.max(jnp.where(token_mask, scores, -jnp.inf), axis=-1))
        weights = jnp.where(token_mask, jnp.exp(scores - local_max[..., None]), 0.0)
        local_sum = lax.optimization_barrier(jnp.sum(weights, axis=-1))
        rounded = lax.optimization_barrier(weights.astype(jnp.bfloat16)).astype(jnp.float32)
        local_out = jnp.einsum('rgqt,tgd->rgqd', rounded, value_part)
        part_out = lax.optimization_barrier((local_out / local_sum[..., None]).astype(jnp.bfloat16)).astype(jnp.float32)
        log_total = local_max + jnp.log(local_sum)
        return (log_total, part_out)
    all_lse, all_part = lax.map(one_shard, jnp.arange(shard_count, dtype=jnp.int32))
    top_lse = lax.optimization_barrier(jnp.max(all_lse, axis=0))
    factor = jnp.exp(all_lse - top_lse[None])
    denominator = lax.optimization_barrier(jnp.sum(factor, axis=0))
    numerator = lax.optimization_barrier(jnp.sum(factor[..., None] * all_part, axis=0))
    result = numerator / denominator[..., None]
    return result.reshape(ROWS, QH * HD).astype(jnp.bfloat16)
```

```python
import functools
import math

import jax
import jax.numpy as jnp
from jax import lax
from jax.experimental import pallas as pl
from jax.experimental.pallas import tpu as pltpu
from jax.sharding import PartitionSpec as P

HD = 128
QPK = 5
BLOCK = 128
LANES = 128
TILE = 256
CHUNK = 256
UNLISTED = -float(2**17)
SCALE = 1.0 / math.sqrt(HD)
EXP2_SCALE = SCALE / math.log(2.0)


def attend_kernel(q_ref, k_ref, v_ref, blocks_ref, out_ref, kp_ref, vp_ref, bias_ref, s_ref, m_ref, top_ref, sum_ref):
    rows = q_ref.shape[0]
    tokens = k_ref.shape[0]
    halves = rows // TILE
    tiles = halves * QPK
    chunks = tokens // CHUNK
    listed = blocks_ref[...]
    ids = lax.broadcasted_iota(jnp.int32, (LANES, rows), 0)
    hit = ids < 0
    for j in range(listed.shape[0]):
        hit = hit | (listed[j : j + 1, :] == ids)
    bias_ref[...] = jnp.where(hit, 0.0, UNLISTED).T.astype(jnp.bfloat16)
    kp_ref[:, :HD] = k_ref[...]
    token = lax.broadcasted_iota(jnp.int32, (tokens, LANES), 0) // BLOCK
    lane = lax.broadcasted_iota(jnp.int32, (tokens, LANES), 1)
    kp_ref[:, HD:] = jnp.where(token == lane, 1.0, 0.0).astype(jnp.bfloat16)
    vp_ref[:, :HD] = v_ref[...]
    vp_ref[:, HD:] = jnp.ones((tokens, LANES), jnp.bfloat16)
    top_ref[...] = jnp.zeros_like(top_ref)
    sum_ref[...] = jnp.ones_like(sum_ref)

    def place(i):
        head = i // halves
        return (
            pl.ds(pl.multiple_of((i % halves) * TILE, TILE), TILE),
            pl.ds(pl.multiple_of(head * HD, HD), HD),
            head,
        )

    def score_start(i):
        at, columns, head = place(i)
        return jnp.concatenate([q_ref[at, columns], bias_ref[at, :]], axis=1)

    def score_chunk(i, c, left, best):
        span = slice(c * CHUNK, (c + 1) * CHUNK)
        s = lax.dot_general(left, kp_ref[span, :], (((1,), (1,)), ((), ())), preferred_element_type=jnp.float32)
        s_ref[i % 2, :, span] = s
        for part in range(CHUNK // LANES):
            piece = s[:, part * LANES : (part + 1) * LANES]
            best = piece if best is None else jnp.maximum(best, piece)
        return best

    def score_end(i, best):
        m_ref[i % 2] = jnp.broadcast_to(jnp.max(best, axis=1, keepdims=True), (TILE, LANES))

    def value_chunk(i, c, best, total):
        span = slice(c * CHUNK, (c + 1) * CHUNK)
        s = s_ref[i % 2, :, span]
        p = jnp.exp2((s - jnp.concatenate([best] * (CHUNK // LANES), axis=1)) * EXP2_SCALE).astype(jnp.bfloat16)
        add = jnp.dot(p, vp_ref[span, :], preferred_element_type=jnp.float32)
        return add if total is None else total + add

    def value_end(i, best, total):
        at, columns, head = place(i)
        weight = total[:, HD:]
        out_ref[at, columns] = (total[:, :HD] / weight).astype(jnp.bfloat16)
        here = lax.broadcasted_iota(jnp.int32, (TILE, LANES), 1) == head
        top_ref[at, :] = jnp.where(here, best, top_ref[at, :])
        sum_ref[at, :] = jnp.where(here, weight, sum_ref[at, :])

    def step(i, with_score, with_value):
        best_now = total = None
        if with_score:
            left = score_start(i)
        if with_value:
            best_before = m_ref[(i - 1) % 2]
        for c in range(chunks):
            if with_score:
                best_now = score_chunk(i, c, left, best_now)
            if with_value:
                total = value_chunk(i - 1, c, best_before, total)
        if with_score:
            score_end(i, best_now)
        if with_value:
            value_end(i - 1, best_before, total)

    step(jnp.int32(0), True, False)

    @pl.loop(1, tiles)
    def _(i):
        step(i, True, True)

    step(jnp.int32(tiles), False, True)

    lse = top_ref[...] * SCALE + jnp.log(sum_ref[...])
    high = lse.astype(jnp.bfloat16).astype(jnp.float32)
    rest = lse - high
    middle = rest.astype(jnp.bfloat16).astype(jnp.float32)
    low = (rest - middle).astype(jnp.bfloat16).astype(jnp.float32)
    packed = high + pltpu.roll(middle, 8, 1) + pltpu.roll(low, 16, 1)
    out_ref[:, QPK * HD :] = packed.astype(jnp.bfloat16)


def attend(query, keys, values, blocks):
    rows = query.shape[0]
    tokens = keys.shape[0]
    width = QPK * HD
    return pl.pallas_call(
        attend_kernel,
        out_shape=jax.ShapeDtypeStruct((rows, width + LANES), jnp.bfloat16),
        in_specs=[pl.BlockSpec(memory_space=pltpu.VMEM)] * 4,
        out_specs=pl.BlockSpec(memory_space=pltpu.VMEM),
        scratch_shapes=[
            pltpu.VMEM((tokens, 2 * HD), jnp.bfloat16),
            pltpu.VMEM((tokens, 2 * HD), jnp.bfloat16),
            pltpu.VMEM((rows, LANES), jnp.bfloat16),
            pltpu.VMEM((2, TILE, tokens), jnp.float32),
            pltpu.VMEM((2, TILE, LANES), jnp.float32),
            pltpu.VMEM((rows, LANES), jnp.float32),
            pltpu.VMEM((rows, LANES), jnp.float32),
        ],
        compiler_params=pltpu.CompilerParams(vmem_limit_bytes=40 * 2**20),
        name="attend",
    )(query, keys, values, blocks)


def combine_kernel(parts_ref, out_ref):
    packed = parts_ref[:, :, QPK * HD :].astype(jnp.float32)
    lse = packed + pltpu.roll(packed, LANES - 8, 2) + pltpu.roll(packed, LANES - 16, 2)
    top = jnp.max(lse, axis=0, keepdims=True)
    factor = jnp.exp(lse - top)
    weight = jnp.sum(factor, axis=0)
    for head in range(QPK):
        columns = slice(head * HD, (head + 1) * HD)
        part = parts_ref[:, :, columns].astype(jnp.float32)
        total = jnp.sum(factor[:, :, head : head + 1] * part, axis=0)
        out_ref[:, columns] = (total / weight[:, head : head + 1]).astype(jnp.bfloat16)


def combine(parts):
    shards, rows, width = parts.shape
    return pl.pallas_call(
        combine_kernel,
        out_shape=jax.ShapeDtypeStruct((rows, QPK * HD), jnp.bfloat16),
        in_specs=[pl.BlockSpec(memory_space=pltpu.VMEM)],
        out_specs=pl.BlockSpec(memory_space=pltpu.VMEM),
        name="combine",
    )(parts)


def per_device(query, keys, values, blocks):
    shards = lax.axis_size("ctx")
    own_rows, width = query.shape
    whole = lax.all_to_all(jnp.broadcast_to(query[None], (shards, own_rows, width)), "ctx", split_axis=0, concat_axis=0)
    whole = whole.reshape(shards * own_rows, width)
    parts = attend(whole, keys, values, blocks[:, 0, :].T)
    parts = lax.all_to_all(parts.reshape(shards, own_rows, -1), "ctx", split_axis=0, concat_axis=0)
    finished = combine(parts)
    return lax.all_to_all(finished, "grp", split_axis=0, concat_axis=1, tiled=True)


def solution(mesh):
    placed = (P("ctx", "grp"), P("ctx", "grp"), P("ctx", "grp"), P(None, "ctx", None))
    return jax.shard_map(
        per_device, mesh=mesh, in_specs=placed, out_specs=P(("ctx", "grp"), None), check_vma=False
    )
```

```python
import math

import jax
import jax.numpy as jnp
from jax import lax
from jax.experimental import pallas as pl
from jax.experimental.pallas import tpu as pltpu
from jax.sharding import Mesh
from jax.sharding import PartitionSpec as P

HD = 128
QPK = 5
BLOCK = 128
DEPTH = 8
ACROSS = 4
LANES = 128
TILE_ROWS = 64
CHUNK = 512
SHIFTS = (0, 2, 1, 3)
UNLISTED = -float(2**17)
SCALE = 1.0 / math.sqrt(HD)
EXP2_SCALE = SCALE / math.log(2.0)


def prepare_kernel(x_ref, blocks_ref, k_ref, v_ref, bias_ref, kept_k_ref, kept_v_ref, hot_ref, arrived):
    copies = [
        pltpu.make_async_copy(k_ref, kept_k_ref, arrived.at[0]),
        pltpu.make_async_copy(v_ref, kept_v_ref, arrived.at[1]),
    ]
    for copy in copies:
        copy.start()
    shifts, rows, _ = bias_ref.shape
    listed = blocks_ref[...]
    total = listed.shape[1]
    own = total // (shifts * DEPTH)
    ids = lax.broadcasted_iota(jnp.int32, (LANES, total), 0)
    hit = ids < 0
    for j in range(listed.shape[0]):
        hit = hit | (listed[j : j + 1, :] == ids)
    bias = jnp.where(hit, 0.0, UNLISTED).T.astype(jnp.bfloat16)
    pieces = [bias[i * own : (i + 1) * own, :] for i in range(total // own)]
    for shift in range(shifts):
        source = lax.rem(x_ref[0] + (shifts - shift), shifts)
        for z in range(DEPTH):
            piece = pieces[z * shifts]
            for x in range(1, shifts):
                piece = jnp.where(source == x, pieces[z * shifts + x], piece)
            bias_ref[shift, z * own : (z + 1) * own, :] = piece
    lane = lax.broadcasted_iota(jnp.int32, (BLOCK, LANES), 1)
    for block in range(hot_ref.shape[0] // BLOCK):
        hot_ref[block * BLOCK : (block + 1) * BLOCK, :] = jnp.where(lane == block, 1.0, 0.0).astype(jnp.bfloat16)
    for copy in copies:
        copy.wait()


def prepare(x, blocks, keys, values, across):
    rows = blocks.shape[1] // across
    tokens = keys.shape[0]
    whole = pl.BlockSpec(memory_space=pltpu.VMEM)
    return pl.pallas_call(
        prepare_kernel,
        out_shape=(
            jax.ShapeDtypeStruct((across, rows, LANES), jnp.bfloat16),
            jax.ShapeDtypeStruct(keys.shape, jnp.bfloat16),
            jax.ShapeDtypeStruct(values.shape, jnp.bfloat16),
            jax.ShapeDtypeStruct((tokens, LANES), jnp.bfloat16),
        ),
        in_specs=[
            pl.BlockSpec(memory_space=pltpu.SMEM),
            whole,
            pl.BlockSpec(memory_space=pltpu.HBM),
            pl.BlockSpec(memory_space=pltpu.HBM),
        ],
        out_specs=(whole, whole, whole, whole),
        scratch_shapes=[pltpu.SemaphoreType.DMA((2,))],
        compiler_params=pltpu.CompilerParams(vmem_limit_bytes=8 * 2**20),
        cost_estimate=pl.CostEstimate(flops=2**20, transcendentals=0, bytes_accessed=4 * 2**20),
        name="prepare",
    )(x, blocks, keys, values)


def pack_lse(lse):
    high = lse.astype(jnp.bfloat16).astype(jnp.float32)
    rest = lse - high
    middle = rest.astype(jnp.bfloat16).astype(jnp.float32)
    low = (rest - middle).astype(jnp.bfloat16).astype(jnp.float32)
    return (high + pltpu.roll(middle, 8, 1) + pltpu.roll(low, 16, 1)).astype(jnp.bfloat16)


def attend_kernel(shift, q_ref, bias_ref, k_ref, hot_ref, v_ref, out_ref, s_ref):
    rows = q_ref.shape[0]
    tokens = k_ref.shape[0]
    tiles = rows // TILE_ROWS
    height = TILE_ROWS * QPK
    chunks = tokens // CHUNK
    ones = jnp.ones((CHUNK, LANES), jnp.bfloat16)
    lefts, bests, tops, totals = {}, {}, {}, {}

    def score_start(i):
        at = slice(i * TILE_ROWS, (i + 1) * TILE_ROWS)
        bias = bias_ref[shift, at, :]
        query = jnp.concatenate([q_ref[at, h * HD : (h + 1) * HD] for h in range(QPK)], axis=0)
        lefts[i] = jnp.concatenate([query, jnp.concatenate([bias] * QPK, axis=0)], axis=1)

    def score_chunk(i, c):
        span = slice(c * CHUNK, (c + 1) * CHUNK)
        right = jnp.concatenate([k_ref[span, :], hot_ref[span, :]], axis=1)
        s = lax.dot_general(lefts[i], right, (((1,), (1,)), ((), ())), preferred_element_type=jnp.float32)
        s_ref[i % 2, :, span] = s
        best = bests.get(i)
        for part in range(CHUNK // LANES):
            piece = s[:, part * LANES : (part + 1) * LANES]
            best = piece if best is None else jnp.maximum(best, piece)
        bests[i] = best

    def score_end(i):
        tops[i] = jnp.broadcast_to(jnp.max(bests[i], axis=1, keepdims=True), (height, LANES))

    def value_chunk(i, c):
        span = slice(c * CHUNK, (c + 1) * CHUNK)
        s = s_ref[i % 2, :, span]
        top = jnp.concatenate([tops[i]] * (CHUNK // LANES), axis=1)
        p = jnp.exp2((s - top) * EXP2_SCALE).astype(jnp.bfloat16)
        add = jnp.dot(p, jnp.concatenate([v_ref[span, :], ones], axis=1), preferred_element_type=jnp.float32)
        totals[i] = totals[i] + add if i in totals else add

    def value_end(i):
        at = slice(i * TILE_ROWS, (i + 1) * TILE_ROWS)
        lane = lax.broadcasted_iota(jnp.int32, (TILE_ROWS, LANES), 1)
        top = jnp.zeros((TILE_ROWS, LANES), jnp.float32)
        weight = jnp.ones((TILE_ROWS, LANES), jnp.float32)
        for h in range(QPK):
            span = slice(h * TILE_ROWS, (h + 1) * TILE_ROWS)
            mass = totals[i][span, HD:]
            out_ref[at, h * HD : (h + 1) * HD] = (totals[i][span, :HD] / mass).astype(jnp.bfloat16)
            top = jnp.where(lane == h, tops[i][span, :], top)
            weight = jnp.where(lane == h, mass, weight)
        out_ref[at, QPK * HD :] = pack_lse(top * SCALE + jnp.log(weight))

    for i in range(tiles + 1):
        if i < tiles:
            score_start(i)
        for c in range(chunks):
            if i < tiles:
                score_chunk(i, c)
            if i > 0:
                value_chunk(i - 1, c)
        if i < tiles:
            score_end(i)
        if i > 0:
            value_end(i - 1)


def group(shift, query, bias, keys, hot, values):
    rows = query.shape[0]
    tokens = keys.shape[0]
    width = QPK * HD
    return pl.pallas_call(
        lambda *refs: attend_kernel(shift, *refs),
        out_shape=jax.ShapeDtypeStruct((rows, width + LANES), jnp.bfloat16),
        in_specs=[pl.BlockSpec(memory_space=pltpu.VMEM)] * 5,
        out_specs=pl.BlockSpec(memory_space=pltpu.VMEM),
        scratch_shapes=[pltpu.VMEM((2, TILE_ROWS * QPK, tokens), jnp.float32)],
        compiler_params=pltpu.CompilerParams(vmem_limit_bytes=20 * 2**20),
        cost_estimate=pl.CostEstimate(
            flops=8 * rows * QPK * tokens * HD, transcendentals=rows * QPK * tokens, bytes_accessed=2 * 2**20
        ),
        name="attend",
    )(query, bias, keys, hot, values)


def unpack_lse(packed):
    packed = packed.astype(jnp.float32)
    axis = packed.ndim - 1
    return packed + pltpu.roll(packed, LANES - 8, axis) + pltpu.roll(packed, LANES - 16, axis)


def merge_kernel(*refs):
    parts, out_ref = refs[:-1], refs[-1]
    width = QPK * HD
    lses = [unpack_lse(ref[:, width:]) for ref in parts]
    top = lses[0]
    for lse in lses[1:]:
        top = jnp.maximum(top, lse)
    factors = [jnp.exp(lse - top) for lse in lses]
    weight = factors[0]
    for factor in factors[1:]:
        weight = weight + factor
    share = [factor / weight for factor in factors]
    for h in range(QPK):
        columns = slice(h * HD, (h + 1) * HD)
        total = None
        for ref, factor in zip(parts, share):
            term = factor[:, h : h + 1] * ref[:, columns].astype(jnp.float32)
            total = term if total is None else total + term
        out_ref[:, columns] = total.astype(jnp.bfloat16)
    lane = lax.broadcasted_iota(jnp.int32, top.shape, 1)
    out_ref[:, width:] = pack_lse(jnp.where(lane < QPK, top + jnp.log(weight), 0.0))


def merge(parts):
    return pl.pallas_call(
        merge_kernel,
        out_shape=jax.ShapeDtypeStruct(parts[0].shape, jnp.bfloat16),
        in_specs=[pl.BlockSpec(memory_space=pltpu.VMEM)] * len(parts),
        out_specs=pl.BlockSpec(memory_space=pltpu.VMEM),
        compiler_params=pltpu.CompilerParams(vmem_limit_bytes=8 * 2**20),
        name="merge",
    )(*parts)


def finish_kernel(parts_ref, out_ref):
    width = QPK * HD
    lse = unpack_lse(parts_ref[:, :, width:])
    top = jnp.max(lse, axis=0, keepdims=True)
    factor = jnp.exp(lse - top)
    weight = jnp.sum(factor, axis=0)
    rows, total_width = out_ref.shape
    for h in range(QPK):
        part = parts_ref[:, :, h * HD : (h + 1) * HD].astype(jnp.float32)
        total = jnp.sum(factor[:, :, h : h + 1] * part, axis=0)
        done = (total / weight[:, h : h + 1]).astype(jnp.bfloat16)
        for g in range(total_width // width):
            out_ref[:, g * width + h * HD : g * width + (h + 1) * HD] = done[g * rows : (g + 1) * rows, :]


def finish(parts, rows):
    shards, grouped, wide = parts.shape
    return pl.pallas_call(
        finish_kernel,
        out_shape=jax.ShapeDtypeStruct((rows, grouped // rows * QPK * HD), jnp.bfloat16),
        in_specs=[pl.BlockSpec(memory_space=pltpu.VMEM)],
        out_specs=pl.BlockSpec(memory_space=pltpu.VMEM),
        compiler_params=pltpu.CompilerParams(vmem_limit_bytes=8 * 2**20),
        name="finish",
    )(parts)


def per_device(query, keys, values, blocks):
    depth, across, groups = lax.axis_size("z"), lax.axis_size("x"), lax.axis_size("grp")
    own_rows, width = query.shape
    rows = depth * own_rows
    x = lax.axis_index("x").reshape(1)
    bias, keys, values, hot = prepare(x, blocks[:, 0, :].T, keys, values, across)
    wide = jnp.broadcast_to(query[None], (depth, own_rows, width))
    column = lax.all_to_all(wide, "z", split_axis=0, concat_axis=0).reshape(rows, width)

    def move(array, shift):
        return lax.ppermute(array, "x", [(i, (i + shift) % across) for i in range(across)])

    queries = {shift: move(column, shift) if shift else column for shift in SHIFTS}
    parts = []
    for shift in SHIFTS:
        part = group(shift, queries[shift], bias, keys, hot, values)
        parts.append(move(part, across - shift) if shift else part)
    merged = merge(parts)
    share = own_rows // groups
    pieces = lax.all_to_all(merged.reshape(depth * groups, share, -1), ("z", "grp"), split_axis=0, concat_axis=0)
    return finish(pieces.reshape(depth, own_rows, -1), share)


def solution(mesh):
    split = Mesh(mesh.devices.reshape(DEPTH, ACROSS, -1), ("z", "x", "grp"))
    ctx = ("z", "x")
    placed = (P(ctx, "grp"), P(ctx, "grp"), P(ctx, "grp"), P(None, ctx, None))
    return jax.shard_map(
        per_device, mesh=split, in_specs=placed, out_specs=P(("z", "x", "grp"), None), check_vma=False
    )
```

```python
import math

import jax
import jax.numpy as jnp
from jax import lax
from jax.experimental import pallas as pl
from jax.experimental.pallas import tpu as pltpu
from jax.sharding import Mesh
from jax.sharding import PartitionSpec as P

HD = 128
QPK = 5
BLOCK = 128
DEPTH = 8
ACROSS = 4
LANES = 128
TILE_ROWS = 64
CHUNK = 512
SHIFTS = (0, 2, 1, 3)
UNLISTED = -float(2**17)
SCALE = 1.0 / math.sqrt(HD)
EXP2_SCALE = SCALE / math.log(2.0)


def prepare_kernel(x_ref, blocks_ref, k_ref, v_ref, bias_ref, kept_k_ref, kept_v_ref, hot_ref, arrived):
    copies = [
        pltpu.make_async_copy(k_ref, kept_k_ref, arrived.at[0]),
        pltpu.make_async_copy(v_ref, kept_v_ref, arrived.at[1]),
    ]
    for copy in copies:
        copy.start()
    shifts, rows, _ = bias_ref.shape
    listed = blocks_ref[...]
    total = listed.shape[1]
    own = total // (shifts * DEPTH)
    ids = lax.broadcasted_iota(jnp.int32, (LANES, total), 0)
    hit = ids < 0
    for j in range(listed.shape[0]):
        hit = hit | (listed[j : j + 1, :] == ids)
    bias = jnp.where(hit, 0.0, UNLISTED).T.astype(jnp.bfloat16)
    pieces = [bias[i * own : (i + 1) * own, :] for i in range(total // own)]
    for shift in range(shifts):
        source = lax.rem(x_ref[0] + (shifts - shift), shifts)
        for z in range(DEPTH):
            piece = pieces[z * shifts]
            for x in range(1, shifts):
                piece = jnp.where(source == x, pieces[z * shifts + x], piece)
            bias_ref[shift, z * own : (z + 1) * own, :] = piece
    lane = lax.broadcasted_iota(jnp.int32, (BLOCK, LANES), 1)
    for block in range(hot_ref.shape[0] // BLOCK):
        hot_ref[block * BLOCK : (block + 1) * BLOCK, :] = jnp.where(lane == block, 1.0, 0.0).astype(jnp.bfloat16)
    for copy in copies:
        copy.wait()


def prepare(x, blocks, keys, values, across):
    rows = blocks.shape[1] // across
    tokens = keys.shape[0]
    whole = pl.BlockSpec(memory_space=pltpu.VMEM)
    return pl.pallas_call(
        prepare_kernel,
        out_shape=(
            jax.ShapeDtypeStruct((across, rows, LANES), jnp.bfloat16),
            jax.ShapeDtypeStruct(keys.shape, jnp.bfloat16),
            jax.ShapeDtypeStruct(values.shape, jnp.bfloat16),
            jax.ShapeDtypeStruct((tokens, LANES), jnp.bfloat16),
        ),
        in_specs=[
            pl.BlockSpec(memory_space=pltpu.SMEM),
            whole,
            pl.BlockSpec(memory_space=pltpu.HBM),
            pl.BlockSpec(memory_space=pltpu.HBM),
        ],
        out_specs=(whole, whole, whole, whole),
        scratch_shapes=[pltpu.SemaphoreType.DMA((2,))],
        compiler_params=pltpu.CompilerParams(vmem_limit_bytes=8 * 2**20),
        cost_estimate=pl.CostEstimate(flops=2**20, transcendentals=0, bytes_accessed=4 * 2**20),
        name="prepare",
    )(
        x,
        blocks,
        pltpu.with_memory_space_constraint(keys, pltpu.HBM),
        pltpu.with_memory_space_constraint(values, pltpu.HBM),
    )


def pack_lse(lse):
    high = lse.astype(jnp.bfloat16).astype(jnp.float32)
    rest = lse - high
    middle = rest.astype(jnp.bfloat16).astype(jnp.float32)
    low = (rest - middle).astype(jnp.bfloat16).astype(jnp.float32)
    return (high + pltpu.roll(middle, 8, 1) + pltpu.roll(low, 16, 1)).astype(jnp.bfloat16)


def attend_kernel(shift, q_ref, bias_ref, k_ref, hot_ref, v_ref, out_ref, s_ref):
    rows = q_ref.shape[0]
    tokens = k_ref.shape[0]
    tiles = rows // TILE_ROWS
    height = TILE_ROWS * QPK
    chunks = tokens // CHUNK
    ones = jnp.ones((CHUNK, LANES), jnp.bfloat16)
    lefts, bests, tops, totals = {}, {}, {}, {}

    def score_start(i):
        at = slice(i * TILE_ROWS, (i + 1) * TILE_ROWS)
        bias = bias_ref[shift, at, :]
        query = jnp.concatenate([q_ref[at, h * HD : (h + 1) * HD] for h in range(QPK)], axis=0)
        lefts[i] = jnp.concatenate([query, jnp.concatenate([bias] * QPK, axis=0)], axis=1)

    def score_chunk(i, c):
        span = slice(c * CHUNK, (c + 1) * CHUNK)
        right = jnp.concatenate([k_ref[span, :], hot_ref[span, :]], axis=1)
        s = lax.dot_general(lefts[i], right, (((1,), (1,)), ((), ())), preferred_element_type=jnp.float32)
        s_ref[i % 2, :, span] = s
        best = bests.get(i)
        for part in range(CHUNK // LANES):
            piece = s[:, part * LANES : (part + 1) * LANES]
            best = piece if best is None else jnp.maximum(best, piece)
        bests[i] = best

    def score_end(i):
        tops[i] = jnp.broadcast_to(jnp.max(bests[i], axis=1, keepdims=True), (height, LANES))

    def value_chunk(i, c):
        span = slice(c * CHUNK, (c + 1) * CHUNK)
        s = s_ref[i % 2, :, span]
        top = jnp.concatenate([tops[i]] * (CHUNK // LANES), axis=1)
        p = jnp.exp2((s - top) * EXP2_SCALE).astype(jnp.bfloat16)
        add = jnp.dot(p, jnp.concatenate([v_ref[span, :], ones], axis=1), preferred_element_type=jnp.float32)
        totals[i] = totals[i] + add if i in totals else add

    def value_end(i):
        at = slice(i * TILE_ROWS, (i + 1) * TILE_ROWS)
        lane = lax.broadcasted_iota(jnp.int32, (TILE_ROWS, LANES), 1)
        top = jnp.zeros((TILE_ROWS, LANES), jnp.float32)
        weight = jnp.ones((TILE_ROWS, LANES), jnp.float32)
        for h in range(QPK):
            span = slice(h * TILE_ROWS, (h + 1) * TILE_ROWS)
            mass = totals[i][span, HD:]
            out_ref[at, h * HD : (h + 1) * HD] = (totals[i][span, :HD] / mass).astype(jnp.bfloat16)
            top = jnp.where(lane == h, tops[i][span, :], top)
            weight = jnp.where(lane == h, mass, weight)
        out_ref[at, QPK * HD :] = pack_lse(top * SCALE + jnp.log(weight))

    for i in range(tiles + 1):
        if i < tiles:
            score_start(i)
        for c in range(chunks):
            if i < tiles:
                score_chunk(i, c)
            if i > 0:
                value_chunk(i - 1, c)
        if i < tiles:
            score_end(i)
        if i > 0:
            value_end(i - 1)


def group(shift, query, bias, keys, hot, values):
    rows = query.shape[0]
    tokens = keys.shape[0]
    width = QPK * HD
    return pl.pallas_call(
        lambda *refs: attend_kernel(shift, *refs),
        out_shape=jax.ShapeDtypeStruct((rows, width + LANES), jnp.bfloat16),
        in_specs=[pl.BlockSpec(memory_space=pltpu.VMEM)] * 5,
        out_specs=pl.BlockSpec(memory_space=pltpu.VMEM),
        scratch_shapes=[pltpu.VMEM((2, TILE_ROWS * QPK, tokens), jnp.float32)],
        compiler_params=pltpu.CompilerParams(vmem_limit_bytes=20 * 2**20),
        cost_estimate=pl.CostEstimate(
            flops=8 * rows * QPK * tokens * HD, transcendentals=rows * QPK * tokens, bytes_accessed=2 * 2**20
        ),
        name="attend",
    )(query, bias, keys, hot, values)


def unpack_lse(packed):
    packed = packed.astype(jnp.float32)
    axis = packed.ndim - 1
    return packed + pltpu.roll(packed, LANES - 8, axis) + pltpu.roll(packed, LANES - 16, axis)


def merge_kernel(*refs):
    parts, out_ref = refs[:-1], refs[-1]
    width = QPK * HD
    lses = [unpack_lse(ref[:, width:]) for ref in parts]
    top = lses[0]
    for lse in lses[1:]:
        top = jnp.maximum(top, lse)
    factors = [jnp.exp(lse - top) for lse in lses]
    weight = factors[0]
    for factor in factors[1:]:
        weight = weight + factor
    share = [factor / weight for factor in factors]
    for h in range(QPK):
        columns = slice(h * HD, (h + 1) * HD)
        total = None
        for ref, factor in zip(parts, share):
            term = factor[:, h : h + 1] * ref[:, columns].astype(jnp.float32)
            total = term if total is None else total + term
        out_ref[:, columns] = total.astype(jnp.bfloat16)
    lane = lax.broadcasted_iota(jnp.int32, top.shape, 1)
    out_ref[:, width:] = pack_lse(jnp.where(lane < QPK, top + jnp.log(weight), 0.0))


def merge(parts):
    return pl.pallas_call(
        merge_kernel,
        out_shape=jax.ShapeDtypeStruct(parts[0].shape, jnp.bfloat16),
        in_specs=[pl.BlockSpec(memory_space=pltpu.VMEM)] * len(parts),
        out_specs=pl.BlockSpec(memory_space=pltpu.VMEM),
        compiler_params=pltpu.CompilerParams(vmem_limit_bytes=8 * 2**20),
        name="merge",
    )(*parts)


def finish_kernel(parts_ref, out_ref):
    width = QPK * HD
    lse = unpack_lse(parts_ref[:, :, width:])
    top = jnp.max(lse, axis=0, keepdims=True)
    factor = jnp.exp(lse - top)
    weight = jnp.sum(factor, axis=0)
    rows, total_width = out_ref.shape
    for h in range(QPK):
        part = parts_ref[:, :, h * HD : (h + 1) * HD].astype(jnp.float32)
        total = jnp.sum(factor[:, :, h : h + 1] * part, axis=0)
        done = (total / weight[:, h : h + 1]).astype(jnp.bfloat16)
        for g in range(total_width // width):
            out_ref[:, g * width + h * HD : g * width + (h + 1) * HD] = done[g * rows : (g + 1) * rows, :]


def finish(parts, rows):
    shards, grouped, wide = parts.shape
    return pl.pallas_call(
        finish_kernel,
        out_shape=jax.ShapeDtypeStruct((rows, grouped // rows * QPK * HD), jnp.bfloat16),
        in_specs=[pl.BlockSpec(memory_space=pltpu.VMEM)],
        out_specs=pl.BlockSpec(memory_space=pltpu.VMEM),
        compiler_params=pltpu.CompilerParams(vmem_limit_bytes=8 * 2**20),
        name="finish",
    )(parts)


def per_device(query, keys, values, blocks):
    depth, across, groups = lax.axis_size("z"), lax.axis_size("x"), lax.axis_size("grp")
    own_rows, width = query.shape
    rows = depth * own_rows
    x = lax.axis_index("x").reshape(1)
    bias, keys, values, hot = prepare(x, blocks[:, 0, :].T, keys, values, across)
    wide = jnp.broadcast_to(query[None], (depth, own_rows, width))
    column = lax.all_to_all(wide, "z", split_axis=0, concat_axis=0).reshape(rows, width)

    def move(array, shift):
        return lax.ppermute(array, "x", [(i, (i + shift) % across) for i in range(across)])

    queries = {shift: move(column, shift) if shift else column for shift in SHIFTS}
    parts = []
    for shift in SHIFTS:
        part = group(shift, queries[shift], bias, keys, hot, values)
        parts.append(move(part, across - shift) if shift else part)
    merged = merge(parts)
    share = own_rows // groups
    pieces = lax.all_to_all(merged.reshape(depth * groups, share, -1), ("z", "grp"), split_axis=0, concat_axis=0)
    return finish(pieces.reshape(depth, own_rows, -1), share)


def solution(mesh):
    split = Mesh(mesh.devices.reshape(DEPTH, ACROSS, -1), ("z", "x", "grp"))
    ctx = ("z", "x")
    placed = (P(ctx, "grp"), P(ctx, "grp"), P(ctx, "grp"), P(None, ctx, None))
    return jax.shard_map(
        per_device, mesh=split, in_specs=placed, out_specs=P(("z", "x", "grp"), None), check_vma=False
    )
```

```python
import math

import jax
import jax.numpy as jnp
from jax import lax
from jax.experimental import pallas as pl
from jax.experimental.pallas import tpu as pltpu
from jax.sharding import Mesh
from jax.sharding import PartitionSpec as P

HD = 128
QPK = 5
BLOCK = 128
DEPTH = 8
ACROSS = 4
LANES = 128
TILE_ROWS = 64
CHUNK = 512
SHIFTS = (0, 1, 2, 3)
UNLISTED = -float(2**17)
SCALE = 1.0 / math.sqrt(HD)
EXP2_SCALE = SCALE / math.log(2.0)


def prepare_kernel(x_ref, blocks_ref, k_ref, v_ref, bias_ref, kept_k_ref, kept_v_ref, hot_ref, arrived):
    copies = [
        pltpu.make_async_copy(k_ref, kept_k_ref, arrived.at[0]),
        pltpu.make_async_copy(v_ref, kept_v_ref, arrived.at[1]),
    ]
    for copy in copies:
        copy.start()
    shifts, rows, _ = bias_ref.shape
    listed = blocks_ref[...]
    total = listed.shape[1]
    own = total // (shifts * DEPTH)
    ids = lax.broadcasted_iota(jnp.int32, (LANES, total), 0)
    hit = ids < 0
    for j in range(listed.shape[0]):
        hit = hit | (listed[j : j + 1, :] == ids)
    bias = jnp.where(hit, 0.0, UNLISTED).T.astype(jnp.bfloat16)
    pieces = [bias[i * own : (i + 1) * own, :] for i in range(total // own)]
    for shift in range(shifts):
        source = lax.rem(x_ref[0] + (shifts - shift), shifts)
        for z in range(DEPTH):
            piece = pieces[z * shifts]
            for x in range(1, shifts):
                piece = jnp.where(source == x, pieces[z * shifts + x], piece)
            bias_ref[shift, z * own : (z + 1) * own, :] = piece
    lane = lax.broadcasted_iota(jnp.int32, (BLOCK, LANES), 1)
    for block in range(hot_ref.shape[0] // BLOCK):
        hot_ref[block * BLOCK : (block + 1) * BLOCK, :] = jnp.where(lane == block, 1.0, 0.0).astype(jnp.bfloat16)
    for copy in copies:
        copy.wait()


def prepare(x, blocks, keys, values, across):
    rows = blocks.shape[1] // across
    tokens = keys.shape[0]
    whole = pl.BlockSpec(memory_space=pltpu.VMEM)
    return pl.pallas_call(
        prepare_kernel,
        out_shape=(
            jax.ShapeDtypeStruct((across, rows, LANES), jnp.bfloat16),
            jax.ShapeDtypeStruct(keys.shape, jnp.bfloat16),
            jax.ShapeDtypeStruct(values.shape, jnp.bfloat16),
            jax.ShapeDtypeStruct((tokens, LANES), jnp.bfloat16),
        ),
        in_specs=[
            pl.BlockSpec(memory_space=pltpu.SMEM),
            whole,
            pl.BlockSpec(memory_space=pltpu.HBM),
            pl.BlockSpec(memory_space=pltpu.HBM),
        ],
        out_specs=(whole, whole, whole, whole),
        scratch_shapes=[pltpu.SemaphoreType.DMA((2,))],
        compiler_params=pltpu.CompilerParams(vmem_limit_bytes=8 * 2**20),
        cost_estimate=pl.CostEstimate(flops=2**20, transcendentals=0, bytes_accessed=4 * 2**20),
        name="prepare",
    )(
        x,
        blocks,
        pltpu.with_memory_space_constraint(keys, pltpu.HBM),
        pltpu.with_memory_space_constraint(values, pltpu.HBM),
    )


def pack_lse(lse):
    high = lse.astype(jnp.bfloat16).astype(jnp.float32)
    rest = lse - high
    middle = rest.astype(jnp.bfloat16).astype(jnp.float32)
    low = (rest - middle).astype(jnp.bfloat16).astype(jnp.float32)
    return (high + pltpu.roll(middle, 8, 1) + pltpu.roll(low, 16, 1)).astype(jnp.bfloat16)


def attend_kernel(shift, q_ref, bias_ref, k_ref, hot_ref, v_ref, out_ref, s_ref):
    rows = q_ref.shape[0]
    tokens = k_ref.shape[0]
    tiles = rows // TILE_ROWS
    height = TILE_ROWS * QPK
    chunks = tokens // CHUNK
    ones = jnp.ones((CHUNK, LANES), jnp.bfloat16)
    lefts, bests, tops, totals = {}, {}, {}, {}

    def score_start(i):
        at = slice(i * TILE_ROWS, (i + 1) * TILE_ROWS)
        bias = bias_ref[shift, at, :]
        query = jnp.concatenate([q_ref[at, h * HD : (h + 1) * HD] for h in range(QPK)], axis=0)
        lefts[i] = jnp.concatenate([query, jnp.concatenate([bias] * QPK, axis=0)], axis=1)

    def score_chunk(i, c):
        span = slice(c * CHUNK, (c + 1) * CHUNK)
        right = jnp.concatenate([k_ref[span, :], hot_ref[span, :]], axis=1)
        s = lax.dot_general(lefts[i], right, (((1,), (1,)), ((), ())), preferred_element_type=jnp.float32)
        s_ref[i % 2, :, span] = s
        best = bests.get(i)
        for part in range(CHUNK // LANES):
            piece = s[:, part * LANES : (part + 1) * LANES]
            best = piece if best is None else jnp.maximum(best, piece)
        bests[i] = best

    def score_end(i):
        tops[i] = jnp.broadcast_to(jnp.max(bests[i], axis=1, keepdims=True), (height, LANES))

    def value_chunk(i, c):
        span = slice(c * CHUNK, (c + 1) * CHUNK)
        s = s_ref[i % 2, :, span]
        top = jnp.concatenate([tops[i]] * (CHUNK // LANES), axis=1)
        p = jnp.exp2((s - top) * EXP2_SCALE).astype(jnp.bfloat16)
        add = jnp.dot(p, jnp.concatenate([v_ref[span, :], ones], axis=1), preferred_element_type=jnp.float32)
        totals[i] = totals[i] + add if i in totals else add

    def value_end(i):
        at = slice(i * TILE_ROWS, (i + 1) * TILE_ROWS)
        lane = lax.broadcasted_iota(jnp.int32, (TILE_ROWS, LANES), 1)
        top = jnp.zeros((TILE_ROWS, LANES), jnp.float32)
        weight = jnp.ones((TILE_ROWS, LANES), jnp.float32)
        for h in range(QPK):
            span = slice(h * TILE_ROWS, (h + 1) * TILE_ROWS)
            mass = totals[i][span, HD:]
            out_ref[at, h * HD : (h + 1) * HD] = (totals[i][span, :HD] / mass).astype(jnp.bfloat16)
            top = jnp.where(lane == h, tops[i][span, :], top)
            weight = jnp.where(lane == h, mass, weight)
        out_ref[at, QPK * HD :] = pack_lse(top * SCALE + jnp.log(weight))

    for i in range(tiles + 1):
        if i < tiles:
            score_start(i)
        for c in range(chunks):
            if i < tiles:
                score_chunk(i, c)
            if i > 0:
                value_chunk(i - 1, c)
        if i < tiles:
            score_end(i)
        if i > 0:
            value_end(i - 1)


def group(shift, query, bias, keys, hot, values):
    rows = query.shape[0]
    tokens = keys.shape[0]
    width = QPK * HD
    return pl.pallas_call(
        lambda *refs: attend_kernel(shift, *refs),
        out_shape=jax.ShapeDtypeStruct((rows, width + LANES), jnp.bfloat16),
        in_specs=[pl.BlockSpec(memory_space=pltpu.VMEM)] * 5,
        out_specs=pl.BlockSpec(memory_space=pltpu.VMEM),
        scratch_shapes=[pltpu.VMEM((2, TILE_ROWS * QPK, tokens), jnp.float32)],
        compiler_params=pltpu.CompilerParams(vmem_limit_bytes=20 * 2**20),
        cost_estimate=pl.CostEstimate(
            flops=8 * rows * QPK * tokens * HD, transcendentals=rows * QPK * tokens, bytes_accessed=2 * 2**20
        ),
        name="attend",
    )(query, bias, keys, hot, values)


def unpack_lse(packed):
    packed = packed.astype(jnp.float32)
    axis = packed.ndim - 1
    return packed + pltpu.roll(packed, LANES - 8, axis) + pltpu.roll(packed, LANES - 16, axis)


def merge_kernel(*refs):
    parts, out_ref = refs[:-1], refs[-1]
    width = QPK * HD
    lses = [unpack_lse(ref[:, width:]) for ref in parts]
    top = lses[0]
    for lse in lses[1:]:
        top = jnp.maximum(top, lse)
    factors = [jnp.exp(lse - top) for lse in lses]
    weight = factors[0]
    for factor in factors[1:]:
        weight = weight + factor
    share = [factor / weight for factor in factors]
    for h in range(QPK):
        columns = slice(h * HD, (h + 1) * HD)
        total = None
        for ref, factor in zip(parts, share):
            term = factor[:, h : h + 1] * ref[:, columns].astype(jnp.float32)
            total = term if total is None else total + term
        out_ref[:, columns] = total.astype(jnp.bfloat16)
    lane = lax.broadcasted_iota(jnp.int32, top.shape, 1)
    out_ref[:, width:] = pack_lse(jnp.where(lane < QPK, top + jnp.log(weight), 0.0))


def merge(parts):
    return pl.pallas_call(
        merge_kernel,
        out_shape=jax.ShapeDtypeStruct(parts[0].shape, jnp.bfloat16),
        in_specs=[pl.BlockSpec(memory_space=pltpu.VMEM)] * len(parts),
        out_specs=pl.BlockSpec(memory_space=pltpu.VMEM),
        compiler_params=pltpu.CompilerParams(vmem_limit_bytes=8 * 2**20),
        name="merge",
    )(*parts)


def finish_kernel(parts_ref, out_ref):
    width = QPK * HD
    lse = unpack_lse(parts_ref[:, :, width:])
    top = jnp.max(lse, axis=0, keepdims=True)
    factor = jnp.exp(lse - top)
    weight = jnp.sum(factor, axis=0)
    rows, total_width = out_ref.shape
    for h in range(QPK):
        part = parts_ref[:, :, h * HD : (h + 1) * HD].astype(jnp.float32)
        total = jnp.sum(factor[:, :, h : h + 1] * part, axis=0)
        done = (total / weight[:, h : h + 1]).astype(jnp.bfloat16)
        for g in range(total_width // width):
            out_ref[:, g * width + h * HD : g * width + (h + 1) * HD] = done[g * rows : (g + 1) * rows, :]


def finish(parts, rows):
    shards, grouped, wide = parts.shape
    return pl.pallas_call(
        finish_kernel,
        out_shape=jax.ShapeDtypeStruct((rows, grouped // rows * QPK * HD), jnp.bfloat16),
        in_specs=[pl.BlockSpec(memory_space=pltpu.VMEM)],
        out_specs=pl.BlockSpec(memory_space=pltpu.VMEM),
        compiler_params=pltpu.CompilerParams(vmem_limit_bytes=8 * 2**20),
        name="finish",
    )(parts)


def per_device(query, keys, values, blocks):
    depth, across, groups = lax.axis_size("z"), lax.axis_size("x"), lax.axis_size("grp")
    own_rows, width = query.shape
    rows = depth * own_rows
    x = lax.axis_index("x").reshape(1)
    bias, keys, values, hot = prepare(x, blocks[:, 0, :].T, keys, values, across)
    wide = jnp.broadcast_to(query[None], (depth, own_rows, width))
    column = lax.all_to_all(wide, "z", split_axis=0, concat_axis=0).reshape(rows, width)

    def move(array, shift):
        return lax.ppermute(array, "x", [(i, (i + shift) % across) for i in range(across)])

    queries = {shift: move(column, shift) if shift else column for shift in SHIFTS}
    parts = []
    for shift in SHIFTS:
        part = group(shift, queries[shift], bias, keys, hot, values)
        parts.append(move(part, across - shift) if shift else part)
    merged = merge(parts)
    share = own_rows // groups
    pieces = lax.all_to_all(merged.reshape(depth * groups, share, -1), ("z", "grp"), split_axis=0, concat_axis=0)
    return finish(pieces.reshape(depth, own_rows, -1), share)


def solution(mesh):
    split = Mesh(mesh.devices.reshape(DEPTH, ACROSS, -1), ("z", "x", "grp"))
    ctx = ("z", "x")
    placed = (P(ctx, "grp"), P(ctx, "grp"), P(ctx, "grp"), P(None, ctx, None))
    return jax.shard_map(
        per_device, mesh=split, in_specs=placed, out_specs=P(("z", "x", "grp"), None), check_vma=False
    )
```

```python
import math

import jax
import jax.numpy as jnp
from jax import lax
from jax.experimental import pallas as pl
from jax.experimental.pallas import tpu as pltpu
from jax.sharding import Mesh
from jax.sharding import PartitionSpec as P

HD = 128
QPK = 5
BLOCK = 128
DEPTH = 8
ACROSS = 4
LANES = 128
TILE_ROWS = 128
CHUNK = 2048
SPAN = 512
SHIFTS = (0, 1, 2, 3)
UNLISTED = -float(2**17)
SCALE = 1.0 / math.sqrt(HD)
EXP2_SCALE = SCALE / math.log(2.0)


def prepare_kernel(x_ref, blocks_ref, k_ref, v_ref, bias_ref, kept_k_ref, kept_v_ref, hot_ref, arrived):
    copies = [
        pltpu.make_async_copy(k_ref, kept_k_ref, arrived.at[0]),
        pltpu.make_async_copy(v_ref, kept_v_ref, arrived.at[1]),
    ]
    for copy in copies:
        copy.start()
    shifts, rows, _ = bias_ref.shape
    listed = blocks_ref[...]
    total = listed.shape[1]
    own = total // (shifts * DEPTH)
    ids = lax.broadcasted_iota(jnp.int32, (LANES, total), 0)
    hit = ids < 0
    for j in range(listed.shape[0]):
        hit = hit | (listed[j : j + 1, :] == ids)
    bias = jnp.where(hit, 0.0, UNLISTED).T.astype(jnp.bfloat16)
    pieces = [bias[i * own : (i + 1) * own, :] for i in range(total // own)]
    for shift in range(shifts):
        source = lax.rem(x_ref[0] + (shifts - shift), shifts)
        for z in range(DEPTH):
            piece = pieces[z * shifts]
            for x in range(1, shifts):
                piece = jnp.where(source == x, pieces[z * shifts + x], piece)
            bias_ref[shift, z * own : (z + 1) * own, :] = piece
    lane = lax.broadcasted_iota(jnp.int32, (BLOCK, LANES), 1)
    for block in range(hot_ref.shape[0] // BLOCK):
        hot_ref[block * BLOCK : (block + 1) * BLOCK, :] = jnp.where(lane == block, 1.0, 0.0).astype(jnp.bfloat16)
    for copy in copies:
        copy.wait()


def prepare(x, blocks, keys, values, across):
    rows = blocks.shape[1] // across
    tokens = keys.shape[0]
    whole = pl.BlockSpec(memory_space=pltpu.VMEM)
    return pl.pallas_call(
        prepare_kernel,
        out_shape=(
            jax.ShapeDtypeStruct((across, rows, LANES), jnp.bfloat16),
            jax.ShapeDtypeStruct(keys.shape, jnp.bfloat16),
            jax.ShapeDtypeStruct(values.shape, jnp.bfloat16),
            jax.ShapeDtypeStruct((tokens, LANES), jnp.bfloat16),
        ),
        in_specs=[
            pl.BlockSpec(memory_space=pltpu.SMEM),
            whole,
            pl.BlockSpec(memory_space=pltpu.HBM),
            pl.BlockSpec(memory_space=pltpu.HBM),
        ],
        out_specs=(whole, whole, whole, whole),
        scratch_shapes=[pltpu.SemaphoreType.DMA((2,))],
        compiler_params=pltpu.CompilerParams(vmem_limit_bytes=8 * 2**20),
        cost_estimate=pl.CostEstimate(flops=2**20, transcendentals=0, bytes_accessed=4 * 2**20),
        name="prepare",
    )(
        x,
        blocks,
        pltpu.with_memory_space_constraint(keys, pltpu.HBM),
        pltpu.with_memory_space_constraint(values, pltpu.HBM),
    )


def pack_lse(lse):
    high = lse.astype(jnp.bfloat16).astype(jnp.float32)
    rest = lse - high
    middle = rest.astype(jnp.bfloat16).astype(jnp.float32)
    low = (rest - middle).astype(jnp.bfloat16).astype(jnp.float32)
    return (high + pltpu.roll(middle, 8, 1) + pltpu.roll(low, 16, 1)).astype(jnp.bfloat16)


def attend_kernel(shift, q_ref, bias_ref, k_ref, hot_ref, v_ref, out_ref, s_ref):
    rows = q_ref.shape[0]
    tokens = k_ref.shape[0]
    height = TILE_ROWS * QPK
    chunks = tokens // CHUNK
    steps = [(i, c) for i in range(rows // TILE_ROWS) for c in range(chunks)]
    ones = jnp.ones((SPAN, LANES), jnp.bfloat16)
    lefts, peaks, tops, totals, fades = {}, {}, {}, {}, {}

    def score_start(i):
        at = slice(i * TILE_ROWS, (i + 1) * TILE_ROWS)
        bias = bias_ref[shift, at, :]
        query = jnp.concatenate([q_ref[at, h * HD : (h + 1) * HD] for h in range(QPK)], axis=0)
        lefts[i] = jnp.concatenate([query, jnp.concatenate([bias] * QPK, axis=0)], axis=1)

    def score_span(n, part):
        i, chunk = steps[n]
        span = slice(chunk * CHUNK + part * SPAN, chunk * CHUNK + (part + 1) * SPAN)
        right = jnp.concatenate([k_ref[span, :], hot_ref[span, :]], axis=1)
        s = lax.dot_general(lefts[i], right, (((1,), (1,)), ((), ())), preferred_element_type=jnp.float32)
        s_ref[n % 2, :, part * SPAN : (part + 1) * SPAN] = s
        best = peaks.get(n)
        for lane in range(SPAN // LANES):
            piece = s[:, lane * LANES : (lane + 1) * LANES]
            best = piece if best is None else jnp.maximum(best, piece)
        peaks[n] = best

    def score_end(n):
        i, chunk = steps[n]
        top = jnp.broadcast_to(jnp.max(peaks[n], axis=1, keepdims=True), (height, LANES))
        if chunk:
            top = jnp.maximum(top, tops[n - 1])
            fades[n] = jnp.exp2((tops[n - 1] - top) * EXP2_SCALE)
        tops[n] = top

    def value_span(n, part):
        i, chunk = steps[n]
        span = slice(chunk * CHUNK + part * SPAN, chunk * CHUNK + (part + 1) * SPAN)
        s = s_ref[n % 2, :, part * SPAN : (part + 1) * SPAN]
        top = jnp.concatenate([tops[n]] * (SPAN // LANES), axis=1)
        p = jnp.exp2((s - top) * EXP2_SCALE).astype(jnp.bfloat16)
        add = jnp.dot(p, jnp.concatenate([v_ref[span, :], ones], axis=1), preferred_element_type=jnp.float32)
        if i not in totals:
            totals[i] = add
        elif part:
            totals[i] = totals[i] + add
        else:
            totals[i] = totals[i] * jnp.concatenate([fades[n]] * 2, axis=1) + add

    def value_end(n):
        i, chunk = steps[n]
        at = slice(i * TILE_ROWS, (i + 1) * TILE_ROWS)
        lane = lax.broadcasted_iota(jnp.int32, (TILE_ROWS, LANES), 1)
        top = jnp.zeros((TILE_ROWS, LANES), jnp.float32)
        weight = jnp.ones((TILE_ROWS, LANES), jnp.float32)
        for h in range(QPK):
            span = slice(h * TILE_ROWS, (h + 1) * TILE_ROWS)
            mass = totals[i][span, HD:]
            out_ref[at, h * HD : (h + 1) * HD] = (totals[i][span, :HD] / mass).astype(jnp.bfloat16)
            top = jnp.where(lane == h, tops[n][span, :], top)
            weight = jnp.where(lane == h, mass, weight)
        out_ref[at, QPK * HD :] = pack_lse(top * SCALE + jnp.log(weight))

    for n in range(len(steps) + 1):
        if n < len(steps) and steps[n][1] == 0:
            score_start(steps[n][0])
        for part in range(CHUNK // SPAN):
            if n < len(steps):
                score_span(n, part)
            if n > 0:
                value_span(n - 1, part)
        if n < len(steps):
            score_end(n)
        if n > 0 and steps[n - 1][1] == chunks - 1:
            value_end(n - 1)


def group(shift, query, bias, keys, hot, values):
    rows = query.shape[0]
    tokens = keys.shape[0]
    width = QPK * HD
    return pl.pallas_call(
        lambda *refs: attend_kernel(shift, *refs),
        out_shape=jax.ShapeDtypeStruct((rows, width + LANES), jnp.bfloat16),
        in_specs=[pl.BlockSpec(memory_space=pltpu.VMEM)] * 5,
        out_specs=pl.BlockSpec(memory_space=pltpu.VMEM),
        scratch_shapes=[pltpu.VMEM((2, TILE_ROWS * QPK, CHUNK), jnp.float32)],
        compiler_params=pltpu.CompilerParams(vmem_limit_bytes=24 * 2**20),
        cost_estimate=pl.CostEstimate(
            flops=8 * rows * QPK * tokens * HD, transcendentals=rows * QPK * tokens, bytes_accessed=2 * 2**20
        ),
        name="attend",
    )(query, bias, keys, hot, values)


def unpack_lse(packed):
    packed = packed.astype(jnp.float32)
    axis = packed.ndim - 1
    return packed + pltpu.roll(packed, LANES - 8, axis) + pltpu.roll(packed, LANES - 16, axis)


def merge_kernel(*refs):
    parts, out_ref = refs[:-1], refs[-1]
    width = QPK * HD
    lses = [unpack_lse(ref[:, width:]) for ref in parts]
    top = lses[0]
    for lse in lses[1:]:
        top = jnp.maximum(top, lse)
    factors = [jnp.exp(lse - top) for lse in lses]
    weight = factors[0]
    for factor in factors[1:]:
        weight = weight + factor
    share = [factor / weight for factor in factors]
    for h in range(QPK):
        columns = slice(h * HD, (h + 1) * HD)
        total = None
        for ref, factor in zip(parts, share):
            term = factor[:, h : h + 1] * ref[:, columns].astype(jnp.float32)
            total = term if total is None else total + term
        out_ref[:, columns] = total.astype(jnp.bfloat16)
    lane = lax.broadcasted_iota(jnp.int32, top.shape, 1)
    out_ref[:, width:] = pack_lse(jnp.where(lane < QPK, top + jnp.log(weight), 0.0))


def merge(parts):
    return pl.pallas_call(
        merge_kernel,
        out_shape=jax.ShapeDtypeStruct(parts[0].shape, jnp.bfloat16),
        in_specs=[pl.BlockSpec(memory_space=pltpu.VMEM)] * len(parts),
        out_specs=pl.BlockSpec(memory_space=pltpu.VMEM),
        compiler_params=pltpu.CompilerParams(vmem_limit_bytes=8 * 2**20),
        name="merge",
    )(*parts)


def finish_kernel(parts_ref, out_ref):
    width = QPK * HD
    lse = unpack_lse(parts_ref[:, :, width:])
    top = jnp.max(lse, axis=0, keepdims=True)
    factor = jnp.exp(lse - top)
    weight = jnp.sum(factor, axis=0)
    rows, total_width = out_ref.shape
    for h in range(QPK):
        part = parts_ref[:, :, h * HD : (h + 1) * HD].astype(jnp.float32)
        total = jnp.sum(factor[:, :, h : h + 1] * part, axis=0)
        done = (total / weight[:, h : h + 1]).astype(jnp.bfloat16)
        for g in range(total_width // width):
            out_ref[:, g * width + h * HD : g * width + (h + 1) * HD] = done[g * rows : (g + 1) * rows, :]


def finish(parts, rows):
    shards, grouped, wide = parts.shape
    return pl.pallas_call(
        finish_kernel,
        out_shape=jax.ShapeDtypeStruct((rows, grouped // rows * QPK * HD), jnp.bfloat16),
        in_specs=[pl.BlockSpec(memory_space=pltpu.VMEM)],
        out_specs=pl.BlockSpec(memory_space=pltpu.VMEM),
        compiler_params=pltpu.CompilerParams(vmem_limit_bytes=8 * 2**20),
        name="finish",
    )(parts)


def per_device(query, keys, values, blocks):
    depth, across, groups = lax.axis_size("z"), lax.axis_size("x"), lax.axis_size("grp")
    own_rows, width = query.shape
    rows = depth * own_rows
    x = lax.axis_index("x").reshape(1)
    bias, keys, values, hot = prepare(x, blocks[:, 0, :].T, keys, values, across)
    wide = jnp.broadcast_to(query[None], (depth, own_rows, width))
    column = lax.all_to_all(wide, "z", split_axis=0, concat_axis=0).reshape(rows, width)

    def move(array, shift):
        return lax.ppermute(array, "x", [(i, (i + shift) % across) for i in range(across)])

    queries = {shift: move(column, shift) if shift else column for shift in SHIFTS}
    parts = []
    for shift in SHIFTS:
        part = group(shift, queries[shift], bias, keys, hot, values)
        parts.append(move(part, across - shift) if shift else part)
    merged = merge(parts)
    share = own_rows // groups
    pieces = lax.all_to_all(merged.reshape(depth * groups, share, -1), ("z", "grp"), split_axis=0, concat_axis=0)
    return finish(pieces.reshape(depth, own_rows, -1), share)


def solution(mesh):
    split = Mesh(mesh.devices.reshape(DEPTH, ACROSS, -1), ("z", "x", "grp"))
    ctx = ("z", "x")
    placed = (P(ctx, "grp"), P(ctx, "grp"), P(ctx, "grp"), P(None, ctx, None))
    return jax.shard_map(
        per_device, mesh=split, in_specs=placed, out_specs=P(("z", "x", "grp"), None), check_vma=False
    )
```

```python
import math

import jax
import jax.numpy as jnp
from jax import lax
from jax.experimental import pallas as pl
from jax.experimental.pallas import tpu as pltpu
from jax.sharding import Mesh
from jax.sharding import PartitionSpec as P

HD = 128
QPK = 5
BLOCK = 128
DEPTH = 8
ACROSS = 4
LANES = 128
TILE_ROWS = 128
CHUNK = 2048
SPAN = 512
SHIFTS = (0, 1, 3, 2)
UNLISTED = -float(2**17)
SCALE = 1.0 / math.sqrt(HD)
EXP2_SCALE = SCALE / math.log(2.0)


def prepare_kernel(x_ref, blocks_ref, k_ref, v_ref, bias_ref, kept_k_ref, kept_v_ref, hot_ref, arrived):
    copies = [
        pltpu.make_async_copy(k_ref, kept_k_ref, arrived.at[0]),
        pltpu.make_async_copy(v_ref, kept_v_ref, arrived.at[1]),
    ]
    for copy in copies:
        copy.start()
    shifts, rows, _ = bias_ref.shape
    listed = blocks_ref[...]
    total = listed.shape[1]
    own = total // (shifts * DEPTH)
    ids = lax.broadcasted_iota(jnp.int32, (LANES, total), 0)
    hit = ids < 0
    for j in range(listed.shape[0]):
        hit = hit | (listed[j : j + 1, :] == ids)
    bias = jnp.where(hit, 0.0, UNLISTED).T.astype(jnp.bfloat16)
    pieces = [bias[i * own : (i + 1) * own, :] for i in range(total // own)]
    for shift in range(shifts):
        source = lax.rem(x_ref[0] + (shifts - shift), shifts)
        for z in range(DEPTH):
            piece = pieces[z * shifts]
            for x in range(1, shifts):
                piece = jnp.where(source == x, pieces[z * shifts + x], piece)
            bias_ref[shift, z * own : (z + 1) * own, :] = piece
    lane = lax.broadcasted_iota(jnp.int32, (BLOCK, LANES), 1)
    for block in range(hot_ref.shape[0] // BLOCK):
        hot_ref[block * BLOCK : (block + 1) * BLOCK, :] = jnp.where(lane == block, 1.0, 0.0).astype(jnp.bfloat16)
    for copy in copies:
        copy.wait()


def prepare(x, blocks, keys, values, across):
    rows = blocks.shape[1] // across
    tokens = keys.shape[0]
    whole = pl.BlockSpec(memory_space=pltpu.VMEM)
    return pl.pallas_call(
        prepare_kernel,
        out_shape=(
            jax.ShapeDtypeStruct((across, rows, LANES), jnp.bfloat16),
            jax.ShapeDtypeStruct(keys.shape, jnp.bfloat16),
            jax.ShapeDtypeStruct(values.shape, jnp.bfloat16),
            jax.ShapeDtypeStruct((tokens, LANES), jnp.bfloat16),
        ),
        in_specs=[
            pl.BlockSpec(memory_space=pltpu.SMEM),
            whole,
            pl.BlockSpec(memory_space=pltpu.HBM),
            pl.BlockSpec(memory_space=pltpu.HBM),
        ],
        out_specs=(whole, whole, whole, whole),
        scratch_shapes=[pltpu.SemaphoreType.DMA((2,))],
        compiler_params=pltpu.CompilerParams(vmem_limit_bytes=8 * 2**20),
        cost_estimate=pl.CostEstimate(flops=2**20, transcendentals=0, bytes_accessed=4 * 2**20),
        name="prepare",
    )(
        x,
        blocks,
        pltpu.with_memory_space_constraint(keys, pltpu.HBM),
        pltpu.with_memory_space_constraint(values, pltpu.HBM),
    )


def pack_lse(lse):
    high = lse.astype(jnp.bfloat16).astype(jnp.float32)
    rest = lse - high
    middle = rest.astype(jnp.bfloat16).astype(jnp.float32)
    low = (rest - middle).astype(jnp.bfloat16).astype(jnp.float32)
    return (high + pltpu.roll(middle, 8, 1) + pltpu.roll(low, 16, 1)).astype(jnp.bfloat16)


def attend_kernel(shift, q_ref, bias_ref, k_ref, hot_ref, v_ref, out_ref, s_ref):
    rows = q_ref.shape[0]
    tokens = k_ref.shape[0]
    height = TILE_ROWS * QPK
    chunks = tokens // CHUNK
    steps = [(i, c) for i in range(rows // TILE_ROWS) for c in range(chunks)]
    ones = jnp.ones((SPAN, LANES), jnp.bfloat16)
    lefts, peaks, tops, totals, fades = {}, {}, {}, {}, {}

    def score_start(i):
        at = slice(i * TILE_ROWS, (i + 1) * TILE_ROWS)
        bias = bias_ref[shift, at, :]
        query = jnp.concatenate([q_ref[at, h * HD : (h + 1) * HD] for h in range(QPK)], axis=0)
        lefts[i] = jnp.concatenate([query, jnp.concatenate([bias] * QPK, axis=0)], axis=1)

    def score_span(n, part):
        i, chunk = steps[n]
        span = slice(chunk * CHUNK + part * SPAN, chunk * CHUNK + (part + 1) * SPAN)
        right = jnp.concatenate([k_ref[span, :], hot_ref[span, :]], axis=1)
        s = lax.dot_general(lefts[i], right, (((1,), (1,)), ((), ())), preferred_element_type=jnp.float32)
        s_ref[n % 2, :, part * SPAN : (part + 1) * SPAN] = s
        best = peaks.get(n)
        for lane in range(SPAN // LANES):
            piece = s[:, lane * LANES : (lane + 1) * LANES]
            best = piece if best is None else jnp.maximum(best, piece)
        peaks[n] = best

    def score_end(n):
        i, chunk = steps[n]
        top = jnp.broadcast_to(jnp.max(peaks[n], axis=1, keepdims=True), (height, LANES))
        if chunk:
            top = jnp.maximum(top, tops[n - 1])
            fades[n] = jnp.exp2((tops[n - 1] - top) * EXP2_SCALE)
        tops[n] = top

    def value_span(n, part):
        i, chunk = steps[n]
        span = slice(chunk * CHUNK + part * SPAN, chunk * CHUNK + (part + 1) * SPAN)
        s = s_ref[n % 2, :, part * SPAN : (part + 1) * SPAN]
        top = jnp.concatenate([tops[n]] * (SPAN // LANES), axis=1)
        p = jnp.exp2((s - top) * EXP2_SCALE).astype(jnp.bfloat16)
        add = jnp.dot(p, jnp.concatenate([v_ref[span, :], ones], axis=1), preferred_element_type=jnp.float32)
        if i not in totals:
            totals[i] = add
        elif part:
            totals[i] = totals[i] + add
        else:
            totals[i] = totals[i] * jnp.concatenate([fades[n]] * 2, axis=1) + add

    def value_end(n):
        i, chunk = steps[n]
        at = slice(i * TILE_ROWS, (i + 1) * TILE_ROWS)
        lane = lax.broadcasted_iota(jnp.int32, (TILE_ROWS, LANES), 1)
        top = jnp.zeros((TILE_ROWS, LANES), jnp.float32)
        weight = jnp.ones((TILE_ROWS, LANES), jnp.float32)
        for h in range(QPK):
            span = slice(h * TILE_ROWS, (h + 1) * TILE_ROWS)
            mass = totals[i][span, HD:]
            out_ref[at, h * HD : (h + 1) * HD] = (totals[i][span, :HD] / mass).astype(jnp.bfloat16)
            top = jnp.where(lane == h, tops[n][span, :], top)
            weight = jnp.where(lane == h, mass, weight)
        out_ref[at, QPK * HD :] = pack_lse(top * SCALE + jnp.log(weight))

    for n in range(len(steps) + 1):
        if n < len(steps) and steps[n][1] == 0:
            score_start(steps[n][0])
        for part in range(CHUNK // SPAN):
            if n < len(steps):
                score_span(n, part)
            if n > 0:
                value_span(n - 1, part)
        if n < len(steps):
            score_end(n)
        if n > 0 and steps[n - 1][1] == chunks - 1:
            value_end(n - 1)


def group(shift, query, bias, keys, hot, values):
    rows = query.shape[0]
    tokens = keys.shape[0]
    width = QPK * HD
    return pl.pallas_call(
        lambda *refs: attend_kernel(shift, *refs),
        out_shape=jax.ShapeDtypeStruct((rows, width + LANES), jnp.bfloat16),
        in_specs=[pl.BlockSpec(memory_space=pltpu.VMEM)] * 5,
        out_specs=pl.BlockSpec(memory_space=pltpu.VMEM),
        scratch_shapes=[pltpu.VMEM((2, TILE_ROWS * QPK, CHUNK), jnp.float32)],
        compiler_params=pltpu.CompilerParams(vmem_limit_bytes=24 * 2**20),
        cost_estimate=pl.CostEstimate(
            flops=8 * rows * QPK * tokens * HD // 4, transcendentals=0, bytes_accessed=2**20 // 4
        ),
        name="attend",
    )(query, bias, keys, hot, values)


def unpack_lse(packed):
    packed = packed.astype(jnp.float32)
    axis = packed.ndim - 1
    return packed + pltpu.roll(packed, LANES - 8, axis) + pltpu.roll(packed, LANES - 16, axis)


def merge_kernel(*refs):
    parts, out_ref = refs[:-1], refs[-1]
    width = QPK * HD
    lses = [unpack_lse(ref[:, width:]) for ref in parts]
    top = lses[0]
    for lse in lses[1:]:
        top = jnp.maximum(top, lse)
    factors = [jnp.exp(lse - top) for lse in lses]
    weight = factors[0]
    for factor in factors[1:]:
        weight = weight + factor
    share = [factor / weight for factor in factors]
    for h in range(QPK):
        columns = slice(h * HD, (h + 1) * HD)
        total = None
        for ref, factor in zip(parts, share):
            term = factor[:, h : h + 1] * ref[:, columns].astype(jnp.float32)
            total = term if total is None else total + term
        out_ref[:, columns] = total.astype(jnp.bfloat16)
    lane = lax.broadcasted_iota(jnp.int32, top.shape, 1)
    out_ref[:, width:] = pack_lse(jnp.where(lane < QPK, top + jnp.log(weight), 0.0))


def merge(parts):
    return pl.pallas_call(
        merge_kernel,
        out_shape=jax.ShapeDtypeStruct(parts[0].shape, jnp.bfloat16),
        in_specs=[pl.BlockSpec(memory_space=pltpu.VMEM)] * len(parts),
        out_specs=pl.BlockSpec(memory_space=pltpu.VMEM),
        compiler_params=pltpu.CompilerParams(vmem_limit_bytes=8 * 2**20),
        name="merge",
    )(*parts)


def finish_kernel(parts_ref, out_ref):
    width = QPK * HD
    lse = unpack_lse(parts_ref[:, :, width:])
    top = jnp.max(lse, axis=0, keepdims=True)
    factor = jnp.exp(lse - top)
    weight = jnp.sum(factor, axis=0)
    rows, total_width = out_ref.shape
    for h in range(QPK):
        part = parts_ref[:, :, h * HD : (h + 1) * HD].astype(jnp.float32)
        total = jnp.sum(factor[:, :, h : h + 1] * part, axis=0)
        done = (total / weight[:, h : h + 1]).astype(jnp.bfloat16)
        for g in range(total_width // width):
            out_ref[:, g * width + h * HD : g * width + (h + 1) * HD] = done[g * rows : (g + 1) * rows, :]


def finish(parts, rows):
    shards, grouped, wide = parts.shape
    return pl.pallas_call(
        finish_kernel,
        out_shape=jax.ShapeDtypeStruct((rows, grouped // rows * QPK * HD), jnp.bfloat16),
        in_specs=[pl.BlockSpec(memory_space=pltpu.VMEM)],
        out_specs=pl.BlockSpec(memory_space=pltpu.VMEM),
        compiler_params=pltpu.CompilerParams(vmem_limit_bytes=8 * 2**20),
        name="finish",
    )(parts)


def per_device(query, keys, values, blocks):
    depth, across, groups = lax.axis_size("z"), lax.axis_size("x"), lax.axis_size("grp")
    own_rows, width = query.shape
    rows = depth * own_rows
    x = lax.axis_index("x").reshape(1)
    bias, keys, values, hot = prepare(x, blocks[:, 0, :].T, keys, values, across)
    wide = jnp.broadcast_to(query[None], (depth, own_rows, width))
    column = lax.all_to_all(wide, "z", split_axis=0, concat_axis=0).reshape(rows, width)

    def move(array, shift):
        return lax.ppermute(array, "x", [(i, (i + shift) % across) for i in range(across)])

    queries = {shift: move(column, shift) if shift else column for shift in SHIFTS}
    parts = []
    for shift in SHIFTS:
        part = group(shift, queries[shift], bias, keys, hot, values)
        parts.append(move(part, across - shift) if shift else part)
    merged = merge(parts)
    share = own_rows // groups
    pieces = lax.all_to_all(merged.reshape(depth * groups, share, -1), ("z", "grp"), split_axis=0, concat_axis=0)
    return finish(pieces.reshape(depth, own_rows, -1), share)


def solution(mesh):
    split = Mesh(mesh.devices.reshape(DEPTH, ACROSS, -1), ("z", "x", "grp"))
    ctx = ("z", "x")
    placed = (P(ctx, "grp"), P(ctx, "grp"), P(ctx, "grp"), P(None, ctx, None))
    return jax.shard_map(
        per_device, mesh=split, in_specs=placed, out_specs=P(("z", "x", "grp"), None), check_vma=False
    )
```
